32 devices in a mesh: order: 4 (over y, x), chan: 8 (over z, core).
Axes of the slice: x: 2, y: 2, z: 4, core: 2. Of those that a mesh axis runs over, the one named last changes fastest.
Arguments:
- grad_out: bfloat16 [3, 256, 720, 1440], P(None, 'chan', 'order'), may hold values from -6 to 6
- legendre: bfloat16 [48, 720, 768], P('order', 'chan'), as said below
- filter_re: float32 [256, 720], P('chan'), may hold values from -6 to 6
- filter_im: float32 [256, 720], P('chan'), may hold values from -6 to 6
- quad_weight: float32 [720], P('order'), may hold values from 0.5 to 2
- pair_order: int32 [48], replicated, may hold values from 0 to 359, as said below
Outputs:
- grad_in: bfloat16 [3, 256, 720, 1440], P(None, 'chan', 'order')
The draws below stay inside these ranges and needn't reach their ends.
Inputs may be any that keep to these rules, and one draw needn't show every extreme that they name: `pair_order`: the values are distinct. Slot j belongs to index j // 12 of order. `legendre`: entries in rows r > 720 of the last dimension are zero.
All inputs are finite; a program needn't handle non-finite values.
Results may differ from the reference program's by a relative error of at most 0.0072.
Values may be sent and summed in bfloat16 or wider, within the bound.
A program may use at most 256 MiB of HBM per device.

```python
import math
import jax
import jax.numpy as jnp
from jax import lax

C = 256
NLAT = 720
NLON = 1440
M = 720
SAMPLES = 3
PAIRS = 48
LROWS = 768


def draw_pair_order(key, part):
    return jax.random.permutation(key, M // 2)[:PAIRS].astype(jnp.int32)


def draw_legendre(key, part):
    values = jax.random.normal(key, (PAIRS, NLAT, LROWS), jnp.float32)
    row_ids = jnp.arange(LROWS, dtype=jnp.int32)
    live = (row_ids <= M).astype(jnp.float32)
    return (values * live[None, None, :] * NLAT ** (-0.5)).astype(jnp.bfloat16)


def steps_of(rng, dims, cuts, smallest, top_value):
    level, own = 1.0, jax.random.fold_in(rng, 6)
    for position, blocks in cuts:
        heights = jnp.exp(jax.random.uniform(jax.random.fold_in(own, position), (blocks,), jnp.float32, smallest / len(cuts), top_value / len(cuts)))
        level = level * jnp.repeat(heights, dims[position] // blocks).reshape([-1 if axis == position else 1 for axis in range(len(dims))])
    return level


def normal_values(rng, shape, scale, reach, pieces=(), held_as=jnp.bfloat16):
    factor_of = steps_of(rng, shape, pieces, -0.22, 0.18) if pieces else 1.0
    entries = jax.random.normal(rng, shape, jnp.float32) * scale * factor_of
    return jnp.minimum(jnp.maximum(entries, -reach), reach).astype(held_as)


def setup_inputs(seed: int = 0) -> dict:
    seeds = jax.random.split(jax.random.key(seed), 7)
    return {
        "grad_out": normal_values(seeds[0], (SAMPLES, C, NLAT, NLON), 1.0, 6.0, ((1, 8), (2, 4))),
        "legendre": draw_legendre(jax.random.fold_in(seeds[6], 71), 0),
        "filter_re": normal_values(seeds[2], (C, M), 1.0, 6.0, ((0, 8),), jnp.float32),
        "filter_im": normal_values(seeds[3], (C, M), 1.0, 6.0, ((0, 8),), jnp.float32),
        "quad_weight": jnp.clip(jnp.exp(math.log(2.0) - 1.3862944 * jax.random.uniform(seeds[4], (NLAT,), jnp.float32) ** steps_of(seeds[4], (NLAT,), ((0, 4),), -0.2, 0.2)), 0.5, 2.0),
        "pair_order": draw_pair_order(jax.random.fold_in(seeds[6], 71), 0),
    }


def basis_tables(pair_order):
    low_order = pair_order.astype(jnp.int32)
    high_order = M - 1 - low_order
    orders = jnp.stack([low_order, low_order, high_order, high_order], axis=1).reshape(-1)
    columns = orders.shape[0]
    parity = jnp.arange(columns, dtype=jnp.int32) % 2
    longitude = jnp.arange(NLON, dtype=jnp.int32)
    phases = (longitude[:, None] * orders[None, :]) % NLON
    angles = phases.astype(jnp.float32) * (2.0 * math.pi / NLON)
    fourier = jnp.where(parity[None, :] == 0, jnp.cos(angles), -jnp.sin(angles))
    factor = jnp.where(orders == 0, 1.0, 2.0).astype(jnp.float32)
    forward = (fourier * factor[None, :]).astype(jnp.bfloat16)
    inverse = fourier.T.astype(jnp.bfloat16)
    return forward, inverse


def spectral_masks(low_order):
    row_ids = jnp.arange(LROWS, dtype=jnp.int32)
    below = row_ids[None, :] < (M - low_order)[:, None]
    degree = jnp.where(below, low_order[:, None] + row_ids[None, :], row_ids[None, :] - 1)
    return below, jnp.clip(degree, 0, M - 1).astype(jnp.int32)


def apply_filter(spectrum, low_order, filter_re, filter_im):
    below, degree = spectral_masks(low_order)
    channels = filter_re.shape[0]
    pairs, rows = degree.shape
    gain_re = jnp.take(filter_re, degree.reshape(-1), axis=1).reshape(channels, pairs, rows)
    gain_im = jnp.take(filter_im, degree.reshape(-1), axis=1).reshape(channels, pairs, rows)
    gain_re = jnp.transpose(gain_re, (1, 2, 0))[:, :, None, :]
    gain_im = jnp.transpose(gain_im, (1, 2, 0))[:, :, None, :]
    inside = below[:, :, None, None]
    former = jnp.where(inside, spectrum[..., 0], spectrum[..., 2])
    latter = jnp.where(inside, spectrum[..., 1], spectrum[..., 3])
    real_part = gain_re * former + gain_im * latter
    imag_part = gain_re * latter - gain_im * former
    keep_mask = inside.astype(real_part.dtype)
    split = jnp.stack([real_part * keep_mask, imag_part * keep_mask,
                       real_part * (1.0 - keep_mask), imag_part * (1.0 - keep_mask)], axis=-1)
    return split.astype(jnp.bfloat16)


def reference(grad_out, legendre, filter_re, filter_im, quad_weight, pair_order):
    forward, inverse = basis_tables(pair_order)

    def transform(sample):
        flat = sample.reshape(C * NLAT, NLON)
        result = jnp.dot(flat, forward, preferred_element_type=jnp.float32).astype(jnp.bfloat16)
        return result.reshape(C, NLAT, PAIRS, 4)

    coeffs = lax.map(transform, grad_out)
    per_slot = jnp.transpose(coeffs, (3, 0, 1, 2, 4))

    def one_slot(inputs):
        table, block, lowest = inputs
        spectrum = jnp.einsum("tr,sctq->rscq", table.astype(jnp.float32), block.astype(jnp.float32))
        split = apply_filter(spectrum[None], lowest[None], filter_re, filter_im)[0]
        synth = jnp.einsum("tr,rscq->sctq", table.astype(jnp.float32), split.astype(jnp.float32))
        return synth.astype(jnp.bfloat16)

    synthesis = lax.map(one_slot, (legendre, per_slot, pair_order.astype(jnp.int32)))
    synthesis = jnp.transpose(synthesis, (1, 2, 3, 0, 4)).reshape(SAMPLES, C * NLAT, PAIRS * 4)

    def back(block):
        return jnp.dot(block, inverse, preferred_element_type=jnp.float32)

    values = lax.map(back, synthesis).reshape(SAMPLES, C, NLAT, NLON)
    scale = quad_weight * (2.0 * math.pi / NLON)
    return (values * scale[None, None, :, None]).astype(jnp.bfloat16)
```

```python
import functools
import math

import jax
import jax.numpy as jnp
from jax import lax
from jax.experimental import pallas as pl
from jax.experimental.pallas import tpu as pltpu
from jax.sharding import PartitionSpec as P

NLON = 1440
M = 720


def step_of(count, most):
    return max(d for d in range(1, most + 1) if count % d == 0)


def basis_tables(pair_order, devices, rows):
    low = pair_order.reshape(devices, -1)
    per = low.shape[1]
    orders = jnp.stack([low, low, M - 1 - low, M - 1 - low], axis=1)
    orders = jnp.pad(orders, ((0, 0), (0, 0), (0, rows - per))).reshape(-1)
    shape = (devices, 4, rows)
    real = (lax.broadcasted_iota(jnp.int32, shape, 1) % 2 == 0).reshape(-1)
    live = (lax.broadcasted_iota(jnp.int32, shape, 2) < per).reshape(-1)
    longitude = jnp.arange(NLON, dtype=jnp.int32)

    def table(phases, real, live):
        angles = (phases % NLON).astype(jnp.float32) * (2.0 * math.pi / NLON)
        values = jnp.where(real, jnp.cos(angles), -jnp.sin(angles))
        return jnp.where(live, values, 0.0)

    inverse = table(orders[:, None] * longitude[None, :], real[:, None], live[:, None])
    factor = jnp.where(orders == 0, 1.0, 2.0).astype(jnp.float32)
    forward = (inverse * factor[:, None]).astype(jnp.bfloat16).T
    return forward, inverse.astype(jnp.bfloat16)


def pair_gains(low_order, filter_re, filter_im, packed_rows):
    both = jnp.concatenate([filter_re, filter_im], axis=0).T
    width = both.shape[1]
    padded = jnp.concatenate([both, jnp.zeros((packed_rows, width), jnp.float32)], axis=0)
    tail = jnp.broadcast_to(both[M - 1 : M], (packed_rows - 1 - M, width))
    shifted = jnp.concatenate([both[:1], both, tail], axis=0)
    row_ids = jnp.arange(packed_rows, dtype=jnp.int32)
    below = row_ids[None, :] < (M - low_order)[:, None]
    gathered = []
    for index in range(low_order.shape[0]):
        upper = lax.dynamic_slice_in_dim(padded, low_order[index], packed_rows, 0)
        gathered.append(jnp.where(below[index][:, None], upper, shifted))
    return jnp.stack(gathered, axis=0)


def forward_kernel(x_ref, table_ref, out_ref, *, devices, rows):
    samples, steps, channels, longitudes = x_ref.shape
    sc = samples * channels
    pieces = [x_ref[s, t] for t in range(steps) for s in range(samples)]
    block = jnp.concatenate(pieces, axis=0)
    coeffs = jnp.dot(block, table_ref[...], preferred_element_type=jnp.float32)
    coeffs = coeffs.astype(jnp.bfloat16)
    for t in range(steps):
        turned = coeffs[t * sc : (t + 1) * sc].T
        for d in range(devices):
            parts = [turned[(4 * d + q) * rows : (4 * d + q + 1) * rows] for q in range(4)]
            out_ref[d, t] = jnp.concatenate(parts, axis=1)


def inverse_kernel(scale_ref, band_ref, table_ref, out_ref):
    devices, steps, rows, lanes = band_ref.shape
    samples, _, channels, longitudes = out_ref.shape
    sc = lanes // 4
    turned = []
    for t in range(steps):
        parts = []
        for d in range(devices):
            block = band_ref[d, t]
            parts += [block[:, q * sc : (q + 1) * sc] for q in range(4)]
        turned.append(jnp.concatenate(parts, axis=0).T)
    block = jnp.concatenate(turned, axis=0)
    values = jnp.dot(block, table_ref[...], preferred_element_type=jnp.float32)
    start = pl.program_id(0) * steps
    for t in range(steps):
        scale = scale_ref[start + t]
        for s in range(samples):
            row = t * sc + s * channels
            out_ref[s, t] = (values[row : row + channels] * scale).astype(jnp.bfloat16)


def middle_kernel(low_ref, legendre_ref, coeffs_ref, gains_ref, out_ref, *, samples):
    legendre = legendre_ref[0]
    packed_rows = legendre.shape[1]
    half = coeffs_ref.shape[2] // 2
    sc = half // 2
    channels = sc // samples
    contract = (((0,), (0,)), ((), ()))
    spectrum = lax.dot_general(legendre, coeffs_ref[0], contract, preferred_element_type=jnp.float32)
    row_ids = lax.broadcasted_iota(jnp.int32, (packed_rows, half), 0)
    inside = row_ids < M - low_ref[pl.program_id(0)]
    own = jnp.where(inside, spectrum[:, :half], spectrum[:, half:])
    other = jnp.concatenate([own[:, sc:], own[:, :sc]], axis=1)
    gains = gains_ref[0]
    gain_re = gains[:, :channels]
    gain_im = gains[:, channels:]
    gain_re = jnp.concatenate([gain_re] * (2 * samples), axis=1)
    gain_im = jnp.concatenate([gain_im] * samples + [-gain_im] * samples, axis=1)
    filtered = gain_re * own + gain_im * other
    zeros = jnp.zeros_like(filtered)
    split = jnp.concatenate([jnp.where(inside, filtered, zeros), jnp.where(inside, zeros, filtered)], axis=1)
    synthesis = jnp.dot(legendre, split.astype(jnp.bfloat16), preferred_element_type=jnp.float32)
    out_ref[0] = synthesis.astype(jnp.bfloat16)


def body(grad_out, legendre, filter_re, filter_im, quad_weight, pair_order, *, devices):
    samples, channels, lat_local, longitudes = grad_out.shape
    pairs_dev, _, packed_rows = legendre.shape
    rows = -(-pairs_dev // 16) * 16
    lanes = 4 * samples * channels
    columns = devices * 4 * rows
    steps = step_of(lat_local, 10)
    whole = lax.all_gather(legendre, "chan", axis=1, tiled=True)
    forward, inverse = basis_tables(pair_order, devices, rows)
    grid_block = pl.BlockSpec((samples, steps, channels, longitudes), lambda i: (0, i, 0, 0))
    band_block = pl.BlockSpec((devices, steps, rows, lanes), lambda i: (0, i, 0, 0))
    params = pltpu.CompilerParams(dimension_semantics=("arbitrary",), vmem_limit_bytes=56 << 20)
    coeffs = pl.pallas_call(
        functools.partial(forward_kernel, devices=devices, rows=rows),
        grid=(lat_local // steps,),
        in_specs=[grid_block, pl.BlockSpec((longitudes, columns), lambda i: (0, 0))],
        out_specs=band_block,
        out_shape=jax.ShapeDtypeStruct((devices, lat_local, rows, lanes), jnp.bfloat16),
        compiler_params=params,
        name="fourier",
    )(jnp.transpose(grad_out, (0, 2, 1, 3)), forward)
    gathered = lax.all_to_all(coeffs, "order", split_axis=0, concat_axis=0, tiled=True)
    latitudes = devices * lat_local
    gathered = gathered.reshape(latitudes, rows, lanes)[:, :pairs_dev]
    gathered = jnp.transpose(gathered, (1, 0, 2))
    start_slot = lax.axis_index("order") * pairs_dev
    low_order = lax.dynamic_slice_in_dim(pair_order, start_slot, pairs_dev)
    gains = pair_gains(low_order, filter_re, filter_im, packed_rows)
    synthesis = pl.pallas_call(
        functools.partial(middle_kernel, samples=samples),
        grid=(pairs_dev,),
        in_specs=[
            pl.BlockSpec(memory_space=pltpu.SMEM),
            pl.BlockSpec((1, latitudes, packed_rows), lambda i: (i, 0, 0)),
            pl.BlockSpec((1, latitudes, lanes), lambda i: (i, 0, 0)),
            pl.BlockSpec((1, packed_rows, 2 * channels), lambda i: (i, 0, 0)),
        ],
        out_specs=pl.BlockSpec((1, latitudes, lanes), lambda i: (i, 0, 0)),
        out_shape=jax.ShapeDtypeStruct((pairs_dev, latitudes, lanes), jnp.bfloat16),
        compiler_params=params,
        name="legendre",
    )(low_order, whole, gathered, gains)
    synthesis = jnp.transpose(synthesis, (1, 0, 2))
    synthesis = jnp.pad(synthesis, ((0, 0), (0, rows - pairs_dev), (0, 0)))
    synthesis = synthesis.reshape(devices, lat_local, rows, lanes)
    band = lax.all_to_all(synthesis, "order", split_axis=0, concat_axis=0, tiled=True)
    scale = quad_weight * (2.0 * math.pi / NLON)
    values = pl.pallas_call(
        inverse_kernel,
        grid=(lat_local // steps,),
        in_specs=[
            pl.BlockSpec(memory_space=pltpu.SMEM),
            band_block,
            pl.BlockSpec((columns, longitudes), lambda i: (0, 0)),
        ],
        out_specs=grid_block,
        out_shape=jax.ShapeDtypeStruct((samples, lat_local, channels, longitudes), jnp.bfloat16),
        compiler_params=params,
        name="fourier_back",
    )(scale, band, inverse)
    return jnp.transpose(values, (0, 2, 1, 3))


def solution(mesh):
    in_specs = (
        P(None, "chan", "order", None),
        P("order", "chan", None),
        P("chan", None),
        P("chan", None),
        P("order"),
        P(),
    )
    out_specs = P(None, "chan", "order", None)
    local = functools.partial(body, devices=mesh.shape["order"])
    return jax.shard_map(local, mesh=mesh, in_specs=in_specs, out_specs=out_specs, check_vma=False)
```
